32 devices in a mesh: groups: 2 (over y), ctx: 4 (over z), mp: 2 (over x), rep: 2 (over core).
Axes of the slice: x: 2, y: 2, z: 4, core: 2. Of those that a mesh axis runs over, the one named last changes fastest.
Arguments:
- lru_in: bfloat16 [2048, 4096], P(('groups', 'ctx', 'mp'), 'rep'), parts along dimension 0, may hold values from -6 to 6
- gate_weights: bfloat16 [2, 16, 256, 256], P(None, 'rep', 'mp'), may hold values from -0.375 to 0.375
- decay_param: float32 [4096], P('rep'), may hold values from 4 to 13
- queries: bfloat16 [2048, 2048], P(('groups', 'ctx', 'mp'), 'rep'), parts along dimension 0, may hold values from -7.5 to 7.5
- keys_values: bfloat16 [2048, 256], P(('groups', 'ctx', 'mp')), parts along dimension 0, may hold values from -4 to 4
Outputs:
- recurrent: bfloat16 [2048, 4096], P(('groups', 'ctx', 'mp'), 'rep'), parts along dimension 0
- attended: bfloat16 [2048, 2048], P(('groups', 'ctx', 'mp'), 'rep'), parts along dimension 0
The draws below stay inside these ranges and needn't reach their ends.
There are 2 independent parts, one for each index of `groups`. The reference program is written for one: setup_inputs(seed, part) draws one part's arguments, and reference() takes and returns one part's arrays. A program takes and returns all parts, laid end to end along the dimension named above; an argument that names none is the same for every part. Nothing has to cross between parts.
All inputs are finite; a program needn't handle non-finite values.
Results may differ from the reference program's by a relative error of at most 0.0048.
Values may be sent and summed in bfloat16 or wider, within the bound.
A program may use at most 64 MiB of HBM per device.

```python
import math
import jax
import jax.numpy as jnp
from jax import lax

LRU = 4096
BW = 256
H = 16
HD = 128
WINDOW = 2048
NB = 16
SEQ = 1024


def draw_queries(key, part):
    sampled = jax.random.truncated_normal(jax.random.fold_in(key, 1), -4.0, 4.0, (SEQ, H, HD), jnp.float32)
    return sampled.reshape(SEQ, H * HD).astype(jnp.bfloat16)


def draw_keys_values(key, part):
    sampled = jax.random.truncated_normal(jax.random.fold_in(key, 2), -4.0, 4.0, (SEQ, 2 * HD), jnp.float32)
    return sampled.astype(jnp.bfloat16)


def level_of(key, extent, pieces, least, high):
    def one(position, blocks):
        draws = jax.random.uniform(jax.random.fold_in(jax.random.fold_in(key, 6), position), (blocks,), jnp.float32, least / len(pieces), high / len(pieces))
        return jnp.repeat(jnp.exp(draws), extent[position] // blocks).reshape((-1,) + (1,) * (len(extent) - position - 1))

    level = one(*pieces[0])
    for cut in pieces[1:]:
        level = level * one(*cut)
    return level


def bell_draw(rng, extent, spread, most, split=(), held_as=jnp.bfloat16):
    entries = jax.random.normal(rng, extent, jnp.float32) * spread
    if len(split) > 0:
        entries = level_of(rng, extent, split, -0.22, 0.18) * entries
    return jnp.clip(entries, min=-most, max=most).astype(held_as)


def setup_inputs(seed: int = 0, part: int = 0) -> dict:
    key_list = jax.random.split(jax.random.key(seed), 6)
    part_splits = jax.random.split(jax.random.fold_in(key_list[5], part), 6)
    return {
        "lru_in": bell_draw(part_splits[0], (SEQ, LRU), 1.0, 6.0, ((0, 8), (1, 2))),
        "gate_weights": bell_draw(key_list[1], (2, NB, BW, BW), BW ** -0.5, 0.375, ((1, 2), (2, 2))),
        "decay_param": jnp.clip(4.0 + 9.0 * jax.random.uniform(key_list[2], (LRU,), jnp.float32) ** level_of(key_list[2], (LRU,), ((0, 2),), -0.2, 0.2), 4.0, 13.0),
        "queries": draw_queries(jax.random.fold_in(jax.random.fold_in(key_list[5], part), 71), part),
        "keys_values": draw_keys_values(jax.random.fold_in(jax.random.fold_in(key_list[5], part), 71), part),
    }


def reference(lru_in, gate_weights, decay_param, queries, keys_values):
    decay_rate = jax.nn.softplus(-decay_param)
    block_rows = math.gcd(SEQ, 512)
    block_total = SEQ // block_rows
    x_blocks = lru_in.reshape(block_total, block_rows, NB, BW)
    weights_wide = gate_weights.astype(jnp.float32)

    def advance_row(state_now, inputs_now):
        state_next = inputs_now[0] * state_now + inputs_now[1]
        return (state_next, state_next)

    def recur_block(state_now, x_block):
        gate_sums = jnp.einsum('tbi,gbio->gtbo', x_block.astype(jnp.float32), weights_wide)
        gate_sums = gate_sums.reshape(2, block_rows, LRU)
        log_decay = -8.0 * decay_rate[None, :] * jax.nn.sigmoid(gate_sums[0])
        driven = jnp.sqrt(-jnp.expm1(2.0 * log_decay)) * jax.nn.sigmoid(gate_sums[1]) * x_block.reshape(block_rows, LRU).astype(jnp.float32)
        decays = jnp.exp(log_decay)
        state_end, states = lax.scan(advance_row, state_now, (decays, driven))
        return (state_end, states.astype(jnp.bfloat16))
    _, states = lax.scan(recur_block, jnp.zeros((LRU,), jnp.float32), x_blocks)
    recurrent = states.reshape(SEQ, LRU)
    score_scale = 1.0 / math.sqrt(HD)
    padded = jnp.concatenate([jnp.zeros((WINDOW, 2 * HD), jnp.bfloat16), keys_values], axis=0)

    def attend(block_index):
        first_row = (block_index * block_rows).astype(jnp.int32)
        context = lax.dynamic_slice_in_dim(padded, first_row, WINDOW + block_rows, 0).astype(jnp.float32)
        query_block = lax.dynamic_slice_in_dim(queries, first_row, block_rows, 0).reshape(block_rows, H, HD).astype(jnp.float32)
        scores = jnp.einsum('thd,kd->htk', query_block, context[:, :HD]) * score_scale
        query_pos = first_row + jnp.arange(block_rows, dtype=jnp.int32)
        key_pos = first_row - WINDOW + jnp.arange(WINDOW + block_rows, dtype=jnp.int32)
        allowed = (key_pos[None, :] >= 0) & (key_pos[None, :] <= query_pos[:, None]) & (key_pos[None, :] > query_pos[:, None] - WINDOW)
        scores = jnp.where(allowed[None, :, :], scores, jnp.float32(-1e+30))
        row_max = lax.optimization_barrier(jnp.max(scores, axis=2, keepdims=True))
        expd = jnp.exp(scores - row_max)
        probabilities = (expd / lax.optimization_barrier(jnp.sum(expd, axis=2, keepdims=True))).astype(jnp.bfloat16)
        result = jnp.einsum('htk,kd->thd', probabilities.astype(jnp.float32), context[:, HD:])
        return result.astype(jnp.bfloat16).reshape(block_rows, H * HD)
    attended = lax.map(attend, jnp.arange(block_total, dtype=jnp.int32)).reshape(SEQ, H * HD)
    return (recurrent, attended)
```

```python
import functools
import math

import jax
import jax.numpy as jnp
from jax import lax
from jax.experimental import pallas as pl
from jax.experimental.pallas import tpu as pltpu
from jax.sharding import PartitionSpec as P

WINDOW = 2048
MESH = pl.DeviceIdType.MESH
F32 = jnp.float32
BF16 = jnp.bfloat16


def kernel(
    sizes,
    x_hbm, w_hbm, decay_ref, q_hbm, kv_hbm,
    rec_ref, att_ref,
    x_ref, wbuf, q_ref, kvbuf, bias, rate, decay_run, state_run, total, totals_in,
    local_sem, kv_send, kv_recv, w_send, w_recv, f_send, f_recv, t_send, t_recv,
):
    G, C, M = sizes
    length = C * M
    rows, width = x_ref.shape
    blocks, bw = wbuf.shape[1], wbuf.shape[4]
    share = blocks // G
    slots = kvbuf.shape[0]
    hd = kvbuf.shape[2] // 2
    heads = q_ref.shape[1] // hd
    g, c, m, r = (lax.axis_index(n) for n in ("groups", "ctx", "mp", "rep"))
    place = c * M + m

    def at(position):
        return (g, position // M, position % M, r)

    loads = [
        pltpu.make_async_copy(kv_hbm, kvbuf.at[0], local_sem.at[0]),
        pltpu.make_async_copy(x_hbm, x_ref, local_sem.at[1]),
        pltpu.make_async_copy(w_hbm, wbuf.at[:, :, m], local_sem.at[2]),
        pltpu.make_async_copy(q_hbm, q_ref, local_sem.at[3]),
    ]
    for load in loads:
        load.start()

    barrier = pltpu.get_barrier_semaphore()

    def greet(d, _):
        pl.semaphore_signal(barrier, inc=1, device_id=at((place + d) % length), device_id_type=MESH)
        return 0

    lax.fori_loop(1, length, greet, 0)
    for d in range(1, G):
        pl.semaphore_signal(barrier, inc=1, device_id=((g + d) % G, c, m, r), device_id_type=MESH)
    pl.semaphore_wait(barrier, length - 1 + G - 1)

    def kv_copy(d):
        return pltpu.make_async_remote_copy(
            src_ref=kv_hbm, dst_ref=kvbuf.at[d],
            send_sem=kv_send.at[d - 1], recv_sem=kv_recv.at[d - 1],
            device_id=at((place + d) % length), device_id_type=MESH,
        )

    def w_copy(d, k):
        b = g * share + k
        return pltpu.make_async_remote_copy(
            src_ref=w_hbm.at[:, b], dst_ref=wbuf.at[:, b, m],
            send_sem=w_send.at[d - 1, k], recv_sem=w_recv.at[d - 1, k],
            device_id=(g, c, (m + d) % M, r), device_id_type=MESH,
        )

    def f_copy(e, d, k):
        b = g * share + k
        piece = wbuf.at[:, b, (m + M - d) % M]
        return pltpu.make_async_remote_copy(
            src_ref=piece, dst_ref=piece,
            send_sem=f_send.at[e - 1, d - 1, k], recv_sem=f_recv.at[e - 1, d - 1, k],
            device_id=((g + e) % G, c, m, r), device_id_type=MESH,
        )

    def f_arrival(e, d, k):
        b = ((g + G - e) % G) * share + k
        piece = wbuf.at[:, b, (m + M - d) % M]
        return pltpu.make_async_remote_copy(
            src_ref=piece, dst_ref=piece,
            send_sem=f_send.at[e - 1, d - 1, k], recv_sem=f_recv.at[e - 1, d - 1, k],
            device_id=((g + e) % G, c, m, r), device_id_type=MESH,
        )

    def w_arrival(d, k):
        b = g * share + k
        return pltpu.make_async_remote_copy(
            src_ref=w_hbm.at[:, b], dst_ref=wbuf.at[:, b, (m + M - d) % M],
            send_sem=w_send.at[d - 1, k], recv_sem=w_recv.at[d - 1, k],
            device_id=(g, c, (m + d) % M, r), device_id_type=MESH,
        )

    for d in range(1, M):
        w_copy(d, 0).start()
    for d in range(1, slots):
        kv_copy(d).start()
    for k in range(1, share):
        for d in range(1, M):
            w_copy(d, k).start()

    e = jnp.exp(-decay_ref[...])
    s = e / (2.0 + e)
    s2 = s * s
    rate[...] = -16.0 * s * (1.0 + s2 * (1.0 / 3.0 + s2 * (1.0 / 5.0)))

    row = lax.broadcasted_iota(jnp.int32, (rows, rows), 0)
    col = lax.broadcasted_iota(jnp.int32, (rows, rows), 1)
    for d in range(slots):
        back = row - col + d * rows
        allowed = (back >= 0) & (back < WINDOW) & (place >= d)
        bias[:, d * rows : (d + 1) * rows] = jnp.where(allowed, 0.0, -1e30).astype(F32)

    groups8 = rows // 8
    sub = lax.broadcasted_iota(jnp.int32, (groups8, 8, bw), 1)

    def gates(b):
        lanes = pl.ds(pl.multiple_of(b * bw, bw), bw)
        xb = x_ref[:, lanes]
        g0 = jnp.dot(xb, wbuf[0, b].reshape(bw, bw), preferred_element_type=F32)
        g1 = jnp.dot(xb, wbuf[1, b].reshape(bw, bw), preferred_element_type=F32)
        y = rate[:, lanes] * jax.nn.sigmoid(g0)
        poly = 1.0 + y * (1 / 2 + y * (1 / 6 + y * (1 / 24 + y * (1 / 120 + y * (1 / 720)))))
        u = y * poly
        a = (1.0 + u).reshape(groups8, 8, bw)
        v = jnp.sqrt(-u * (2.0 + u)) * jax.nn.sigmoid(g1) * xb.astype(F32)
        v = v.reshape(groups8, 8, bw)
        for shift in (1, 2, 4):
            keep = sub >= shift
            before_v = jnp.where(keep, pltpu.roll(v, shift, 1), 0.0)
            before_a = jnp.where(keep, pltpu.roll(a, shift, 1), 1.0)
            v = a * before_v + v
            a = a * before_a
        decay_run[:, lanes] = a.reshape(rows, bw)
        state_run[:, lanes] = v.reshape(rows, bw)
        ta, tv = a[0, 7:8], v[0, 7:8]
        for k in range(1, groups8):
            tv = a[k, 7:8] * tv + v[k, 7:8]
            ta = a[k, 7:8] * ta
        total[0:1, lanes] = ta
        total[1:2, lanes] = tv

    scale = 1.0 / math.sqrt(hd)

    def head(h):
        lanes = pl.ds(pl.multiple_of(h * hd, hd), hd)
        keys = kvbuf[:, :, :hd].reshape(slots * rows, hd)
        values = kvbuf[:, :, hd:].reshape(slots * rows, hd)
        scores = lax.dot_general(
            q_ref[:, lanes], keys, (((1,), (1,)), ((), ())), preferred_element_type=F32
        )
        scores = scores * scale + bias[...]
        top = jnp.max(scores, axis=1, keepdims=True)
        weights = jnp.exp(scores - top)
        norm = jnp.sum(weights, axis=1, keepdims=True)
        out = jnp.dot(weights.astype(BF16), values, preferred_element_type=F32)
        att_ref[:, lanes] = (out / norm).astype(BF16)

    loads[1].wait()
    loads[2].wait()

    def direct(k, _):
        for d in range(1, M):
            w_arrival(d, k).wait_recv()
            for e in range(1, G):
                f_copy(e, d, k).start()
        gates(g * share + k)
        return 0

    lax.fori_loop(0, share, direct, 0)

    loads[0].wait()
    loads[3].wait()
    for d in range(1, slots):
        kv_copy(d).wait_recv()

    stages = share * (G - 1)
    early = min(heads // 2, stages)

    def early_head(h, _):
        head(h)
        return 0

    for e in range(1, G):
        def relayed(k, _, e=e):
            stage = (e - 1) * share + k

            @pl.when(stage < early)
            def _():
                head(stage)

            for d in range(1, M):
                f_arrival(e, d, k).wait_recv()
            gates(((g + G - e) % G) * share + k)
            return 0

        lax.fori_loop(0, share, relayed, 0)

    def t_copy(d):
        return pltpu.make_async_remote_copy(
            src_ref=total, dst_ref=totals_in.at[d - 1],
            send_sem=t_send.at[d - 1], recv_sem=t_recv.at[d - 1],
            device_id=at((place + d) % length), device_id_type=MESH,
        )

    def t_start(d, _):
        t_copy(d).start()
        return 0

    lax.fori_loop(1, length, t_start, 0)
    lax.fori_loop(early, heads, early_head, 0)

    def t_fold(i, entering):
        d = length - 1 - i
        t_copy(d).wait_recv()
        new = totals_in[d - 1, 0:1] * entering + totals_in[d - 1, 1:2]
        return jnp.where(place >= d, new, entering)

    entering = lax.fori_loop(0, length - 1, t_fold, jnp.zeros((1, width), F32))

    def finish(k, entering):
        pieces = []
        for half in range(2):
            here = pl.ds(pl.multiple_of(k * 16 + half * 8, 8), 8)
            state = state_run[here] + decay_run[here] * entering
            entering = state[7:8]
            pieces.append(state)
        rec_ref[pl.ds(pl.multiple_of(k * 16, 16), 16)] = jnp.concatenate(pieces, axis=0).astype(BF16)
        return entering

    lax.fori_loop(0, rows // 16, finish, entering)

    for d in range(1, slots):
        kv_copy(d).wait_send()

    def w_sent(k, _):
        for d in range(1, M):
            w_copy(d, k).wait_send()
            for e in range(1, G):
                f_copy(e, d, k).wait_send()
        return 0

    lax.fori_loop(0, share, w_sent, 0)

    def t_sent(d, _):
        t_copy(d).wait_send()
        return 0

    lax.fori_loop(1, length, t_sent, 0)


def on_device(lru_in, gate_weights, decay_param, queries, keys_values):
    G, C, M = (lax.axis_size(n) for n in ("groups", "ctx", "mp"))
    length = C * M
    rows, width = lru_in.shape
    _, blocks, depth, bw = gate_weights.shape
    share = blocks // G
    reach = min(WINDOW // rows, length - 1)
    slots = reach + 1
    dma = pltpu.SemaphoreType.DMA
    anywhere = pl.BlockSpec(memory_space=pl.ANY)
    vmem = pl.BlockSpec(memory_space=pltpu.VMEM)
    return pl.pallas_call(
        functools.partial(kernel, (G, C, M)),
        out_shape=(
            jax.ShapeDtypeStruct(lru_in.shape, BF16),
            jax.ShapeDtypeStruct(queries.shape, BF16),
        ),
        in_specs=[anywhere, anywhere, vmem, anywhere, anywhere],
        out_specs=(vmem, vmem),
        scratch_shapes=[
            pltpu.VMEM((rows, width), BF16),
            pltpu.VMEM((2, blocks, M, depth, bw), BF16),
            pltpu.VMEM(queries.shape, BF16),
            pltpu.VMEM((slots,) + keys_values.shape, BF16),
            pltpu.VMEM((rows, slots * rows), F32),
            pltpu.VMEM((1, width), F32),
            pltpu.VMEM((rows, width), F32),
            pltpu.VMEM((rows, width), F32),
            pltpu.VMEM((2, width), F32),
            pltpu.VMEM((length - 1, 2, width), F32),
            dma((4,)),
            dma((reach,)),
            dma((reach,)),
            dma((M - 1, share)),
            dma((M - 1, share)),
            dma((G - 1, M - 1, share)),
            dma((G - 1, M - 1, share)),
            dma((length - 1,)),
            dma((length - 1,)),
        ],
        compiler_params=pltpu.CompilerParams(
            collective_id=0, has_side_effects=True, vmem_limit_bytes=48 * 2**20
        ),
    )(lru_in, gate_weights, decay_param.reshape(1, width), queries, keys_values)


def solution(mesh):
    in_specs = (
        P(("groups", "ctx", "mp"), "rep"),
        P(None, "rep", "mp", None),
        P("rep"),
        P(("groups", "ctx", "mp"), "rep"),
        P(("groups", "ctx", "mp"), None),
    )
    out_specs = (P(("groups", "ctx", "mp"), "rep"), P(("groups", "ctx", "mp"), "rep"))
    return jax.shard_map(
        on_device, mesh=mesh, in_specs=in_specs, out_specs=out_specs, check_vma=False
    )
```

```python
import functools
import math

import jax
import jax.numpy as jnp
from jax import lax
from jax.experimental import pallas as pl
from jax.experimental.pallas import tpu as pltpu
from jax.sharding import PartitionSpec as P

WINDOW = 2048
MESH = pl.DeviceIdType.MESH
F32 = jnp.float32
BF16 = jnp.bfloat16


def kernel(
    sizes,
    x_hbm, w_hbm, decay_ref, q_hbm, kv_hbm,
    rec_ref, att_ref,
    x_ref, wbuf, q_ref, kvbuf, bias, rate, decay_run, state_run, total, totals_in,
    local_sem, kv_send, kv_recv, w_send, w_recv, f_send, f_recv, t_send, t_recv, r_send, r_recv,
):
    G, C, M, R = sizes
    length = C * M
    rows, width = x_ref.shape
    blocks, bw = wbuf.shape[1], wbuf.shape[4]
    share = blocks // G
    slots = kvbuf.shape[0]
    hd = kvbuf.shape[2] // 2
    heads = q_ref.shape[1] // hd
    g, c, m, r = (lax.axis_index(n) for n in ("groups", "ctx", "mp", "rep"))
    place = c * M + m

    def at(position):
        return (g, position // M, position % M, r)

    loads = [
        pltpu.make_async_copy(kv_hbm, kvbuf.at[0], local_sem.at[0]),
        pltpu.make_async_copy(x_hbm, x_ref, local_sem.at[1]),
        pltpu.make_async_copy(w_hbm, wbuf.at[:, :, m], local_sem.at[2]),
        pltpu.make_async_copy(q_hbm, q_ref, local_sem.at[3]),
    ]
    for load in loads:
        load.start()

    barrier = pltpu.get_barrier_semaphore()

    def greet(d, _):
        pl.semaphore_signal(barrier, inc=1, device_id=at((place + d) % length), device_id_type=MESH)
        return 0

    lax.fori_loop(1, length, greet, 0)
    for d in range(1, G):
        pl.semaphore_signal(barrier, inc=1, device_id=((g + d) % G, c, m, r), device_id_type=MESH)
    for d in range(1, R):
        pl.semaphore_signal(barrier, inc=1, device_id=(g, c, m, (r + d) % R), device_id_type=MESH)
    pl.semaphore_wait(barrier, length - 1 + G - 1 + R - 1)
    part = rows // R
    mine = pl.ds(pl.multiple_of(r * part, part), part)

    def kv_copy(d):
        return pltpu.make_async_remote_copy(
            src_ref=kv_hbm.at[mine], dst_ref=kvbuf.at[d, mine],
            send_sem=kv_send.at[d - 1], recv_sem=kv_recv.at[d - 1],
            device_id=at((place + d) % length), device_id_type=MESH,
        )

    def r_copy(e, d, back=0):
        owner = (r + R - back) % R
        piece = kvbuf.at[d, pl.ds(pl.multiple_of(owner * part, part), part)]
        return pltpu.make_async_remote_copy(
            src_ref=piece, dst_ref=piece,
            send_sem=r_send.at[e - 1, d - 1], recv_sem=r_recv.at[e - 1, d - 1],
            device_id=(g, c, m, (r + e) % R), device_id_type=MESH,
        )

    def w_copy(d, k):
        b = g * share + k
        return pltpu.make_async_remote_copy(
            src_ref=w_hbm.at[:, b], dst_ref=wbuf.at[:, b, m],
            send_sem=w_send.at[d - 1, k], recv_sem=w_recv.at[d - 1, k],
            device_id=(g, c, (m + d) % M, r), device_id_type=MESH,
        )

    def f_copy(e, d, k):
        b = g * share + k
        piece = wbuf.at[:, b, (m + M - d) % M]
        return pltpu.make_async_remote_copy(
            src_ref=piece, dst_ref=piece,
            send_sem=f_send.at[e - 1, d - 1, k], recv_sem=f_recv.at[e - 1, d - 1, k],
            device_id=((g + e) % G, c, m, r), device_id_type=MESH,
        )

    def f_arrival(e, d, k):
        b = ((g + G - e) % G) * share + k
        piece = wbuf.at[:, b, (m + M - d) % M]
        return pltpu.make_async_remote_copy(
            src_ref=piece, dst_ref=piece,
            send_sem=f_send.at[e - 1, d - 1, k], recv_sem=f_recv.at[e - 1, d - 1, k],
            device_id=((g + e) % G, c, m, r), device_id_type=MESH,
        )

    def w_arrival(d, k):
        b = g * share + k
        return pltpu.make_async_remote_copy(
            src_ref=w_hbm.at[:, b], dst_ref=wbuf.at[:, b, (m + M - d) % M],
            send_sem=w_send.at[d - 1, k], recv_sem=w_recv.at[d - 1, k],
            device_id=(g, c, (m + d) % M, r), device_id_type=MESH,
        )

    for d in range(1, M):
        w_copy(d, 0).start()
    for d in range(1, slots):
        kv_copy(d).start()
    for k in range(1, share):
        for d in range(1, M):
            w_copy(d, k).start()

    e = jnp.exp(-decay_ref[...])
    s = e / (2.0 + e)
    s2 = s * s
    rate[...] = -16.0 * s * (1.0 + s2 * (1.0 / 3.0 + s2 * (1.0 / 5.0)))

    row = lax.broadcasted_iota(jnp.int32, (rows, rows), 0)
    col = lax.broadcasted_iota(jnp.int32, (rows, rows), 1)
    for d in range(slots):
        back = row - col + d * rows
        allowed = (back >= 0) & (back < WINDOW) & (place >= d)
        bias[:, d * rows : (d + 1) * rows] = jnp.where(allowed, 0.0, -1e30).astype(F32)

    groups8 = rows // 8
    sub = lax.broadcasted_iota(jnp.int32, (groups8, 8, bw), 1)

    def gates(b):
        lanes = pl.ds(pl.multiple_of(b * bw, bw), bw)
        xb = x_ref[:, lanes]
        g0 = jnp.dot(xb, wbuf[0, b].reshape(bw, bw), preferred_element_type=F32)
        g1 = jnp.dot(xb, wbuf[1, b].reshape(bw, bw), preferred_element_type=F32)
        y = rate[:, lanes] * jax.nn.sigmoid(g0)
        poly = 1.0 + y * (1 / 2 + y * (1 / 6 + y * (1 / 24 + y * (1 / 120 + y * (1 / 720)))))
        u = y * poly
        a = (1.0 + u).reshape(groups8, 8, bw)
        v = jnp.sqrt(-u * (2.0 + u)) * jax.nn.sigmoid(g1) * xb.astype(F32)
        v = v.reshape(groups8, 8, bw)
        for shift in (1, 2, 4):
            keep = sub >= shift
            before_v = jnp.where(keep, pltpu.roll(v, shift, 1), 0.0)
            before_a = jnp.where(keep, pltpu.roll(a, shift, 1), 1.0)
            v = a * before_v + v
            a = a * before_a
        decay_run[:, lanes] = a.reshape(rows, bw)
        state_run[:, lanes] = v.reshape(rows, bw)
        ta, tv = a[0, 7:8], v[0, 7:8]
        for k in range(1, groups8):
            tv = a[k, 7:8] * tv + v[k, 7:8]
            ta = a[k, 7:8] * ta
        total[0:1, lanes] = ta
        total[1:2, lanes] = tv

    scale = 1.0 / math.sqrt(hd)

    def head(h):
        lanes = pl.ds(pl.multiple_of(h * hd, hd), hd)
        keys = kvbuf[:, :, :hd].reshape(slots * rows, hd)
        values = kvbuf[:, :, hd:].reshape(slots * rows, hd)
        scores = lax.dot_general(
            q_ref[:, lanes], keys, (((1,), (1,)), ((), ())), preferred_element_type=F32
        )
        scores = scores * scale + bias[...]
        top = jnp.max(scores, axis=1, keepdims=True)
        weights = jnp.exp(scores - top)
        norm = jnp.sum(weights, axis=1, keepdims=True)
        out = jnp.dot(weights.astype(BF16), values, preferred_element_type=F32)
        att_ref[:, lanes] = (out / norm).astype(BF16)

    loads[1].wait()
    loads[2].wait()

    def direct(k, _):
        for d in range(1, M):
            w_arrival(d, k).wait_recv()
            for e in range(1, G):
                f_copy(e, d, k).start()
        gates(g * share + k)
        return 0

    lax.fori_loop(0, share // 2, direct, 0)
    for d in range(1, slots):
        kv_copy(d).wait_recv()
        for e in range(1, R):
            r_copy(e, d).start()
    lax.fori_loop(share // 2, share, direct, 0)

    loads[0].wait()
    loads[3].wait()
    for d in range(1, slots):
        for e in range(1, R):
            r_copy(e, d, e).wait_recv()

    stages = share * (G - 1)
    early = min(heads // 2, stages)

    def early_head(h, _):
        head(h)
        return 0

    for e in range(1, G):
        def relayed(k, _, e=e):
            stage = (e - 1) * share + k

            @pl.when(stage < early)
            def _():
                head(stage)

            for d in range(1, M):
                f_arrival(e, d, k).wait_recv()
            gates(((g + G - e) % G) * share + k)
            return 0

        lax.fori_loop(0, share, relayed, 0)

    def t_copy(d):
        return pltpu.make_async_remote_copy(
            src_ref=total, dst_ref=totals_in.at[d - 1],
            send_sem=t_send.at[d - 1], recv_sem=t_recv.at[d - 1],
            device_id=at((place + d) % length), device_id_type=MESH,
        )

    def t_start(d, _):
        t_copy(d).start()
        return 0

    lax.fori_loop(1, length, t_start, 0)
    lax.fori_loop(early, heads, early_head, 0)

    def t_fold(i, entering):
        d = length - 1 - i
        t_copy(d).wait_recv()
        new = totals_in[d - 1, 0:1] * entering + totals_in[d - 1, 1:2]
        return jnp.where(place >= d, new, entering)

    entering = lax.fori_loop(0, length - 1, t_fold, jnp.zeros((1, width), F32))

    def finish(k, entering):
        pieces = []
        for half in range(2):
            here = pl.ds(pl.multiple_of(k * 16 + half * 8, 8), 8)
            state = state_run[here] + decay_run[here] * entering
            entering = state[7:8]
            pieces.append(state)
        rec_ref[pl.ds(pl.multiple_of(k * 16, 16), 16)] = jnp.concatenate(pieces, axis=0).astype(BF16)
        return entering

    lax.fori_loop(0, rows // 16, finish, entering)

    for d in range(1, slots):
        kv_copy(d).wait_send()
        for e in range(1, R):
            r_copy(e, d).wait_send()

    def w_sent(k, _):
        for d in range(1, M):
            w_copy(d, k).wait_send()
            for e in range(1, G):
                f_copy(e, d, k).wait_send()
        return 0

    lax.fori_loop(0, share, w_sent, 0)

    def t_sent(d, _):
        t_copy(d).wait_send()
        return 0

    lax.fori_loop(1, length, t_sent, 0)


def on_device(lru_in, gate_weights, decay_param, queries, keys_values):
    G, C, M, R = (lax.axis_size(n) for n in ("groups", "ctx", "mp", "rep"))
    length = C * M
    rows, width = lru_in.shape
    _, blocks, depth, bw = gate_weights.shape
    share = blocks // G
    reach = min(WINDOW // rows, length - 1)
    slots = reach + 1
    dma = pltpu.SemaphoreType.DMA
    anywhere = pl.BlockSpec(memory_space=pltpu.HBM)
    vmem = pl.BlockSpec(memory_space=pltpu.VMEM)
    return pl.pallas_call(
        functools.partial(kernel, (G, C, M, R)),
        out_shape=(
            jax.ShapeDtypeStruct(lru_in.shape, BF16),
            jax.ShapeDtypeStruct(queries.shape, BF16),
        ),
        in_specs=[anywhere, anywhere, vmem, anywhere, anywhere],
        out_specs=(vmem, vmem),
        scratch_shapes=[
            pltpu.VMEM((rows, width), BF16),
            pltpu.VMEM((2, blocks, M, depth, bw), BF16),
            pltpu.VMEM(queries.shape, BF16),
            pltpu.VMEM((slots,) + keys_values.shape, BF16),
            pltpu.VMEM((rows, slots * rows), F32),
            pltpu.VMEM((1, width), F32),
            pltpu.VMEM((rows, width), F32),
            pltpu.VMEM((rows, width), F32),
            pltpu.VMEM((2, width), F32),
            pltpu.VMEM((length - 1, 2, width), F32),
            dma((4,)),
            dma((reach,)),
            dma((reach,)),
            dma((M - 1, share)),
            dma((M - 1, share)),
            dma((G - 1, M - 1, share)),
            dma((G - 1, M - 1, share)),
            dma((length - 1,)),
            dma((length - 1,)),
            dma((R - 1, reach)),
            dma((R - 1, reach)),
        ],
        compiler_params=pltpu.CompilerParams(
            collective_id=0, has_side_effects=True, vmem_limit_bytes=64 * 2**20 - 917504
        ),
    )(lru_in, gate_weights, decay_param.reshape(1, width), queries, keys_values)


def solution(mesh):
    in_specs = (
        P(("groups", "ctx", "mp"), "rep"),
        P(None, "rep", "mp", None),
        P("rep"),
        P(("groups", "ctx", "mp"), "rep"),
        P(("groups", "ctx", "mp"), None),
    )
    out_specs = (P(("groups", "ctx", "mp"), "rep"), P(("groups", "ctx", "mp"), "rep"))
    return jax.shard_map(
        on_device, mesh=mesh, in_specs=in_specs, out_specs=out_specs, check_vma=False
    )
```

```python
import functools
import math

import jax
import jax.numpy as jnp
from jax import lax
from jax.experimental import pallas as pl
from jax.experimental.pallas import tpu as pltpu
from jax.sharding import PartitionSpec as P

WINDOW = 2048
MESH = pl.DeviceIdType.MESH
F32 = jnp.float32
BF16 = jnp.bfloat16


def kernel(
    sizes,
    x_hbm, w_hbm, decay_ref, q_hbm, kv_hbm,
    rec_ref, att_ref,
    x_ref, wbuf, q_ref, kvbuf, bias, rate, decay_run, state_run, total, totals_in,
    local_sem, kv_send, kv_recv, w_send, w_recv, f_send, f_recv, t_send, t_recv, r_send, r_recv,
):
    G, C, M, R = sizes
    length = C * M
    rows, width = x_ref.shape
    blocks, bw = wbuf.shape[1], wbuf.shape[4]
    share = blocks // G
    slots = kvbuf.shape[0]
    hd = kvbuf.shape[2] // 2
    heads = q_ref.shape[1] // hd
    g, c, m, r = (lax.axis_index(n) for n in ("groups", "ctx", "mp", "rep"))
    place = c * M + m

    def at(position):
        return (g, position // M, position % M, r)

    loads = [
        pltpu.make_async_copy(kv_hbm, kvbuf.at[0], local_sem.at[0]),
        pltpu.make_async_copy(x_hbm, x_ref, local_sem.at[1]),
        pltpu.make_async_copy(w_hbm, wbuf.at[:, :, m], local_sem.at[2]),
        pltpu.make_async_copy(q_hbm, q_ref, local_sem.at[3]),
    ]
    for load in loads:
        load.start()

    barrier = pltpu.get_barrier_semaphore()

    def greet(d, _):
        pl.semaphore_signal(barrier, inc=1, device_id=at((place + d) % length), device_id_type=MESH)
        return 0

    lax.fori_loop(1, length, greet, 0)
    for d in range(1, G):
        pl.semaphore_signal(barrier, inc=1, device_id=((g + d) % G, c, m, r), device_id_type=MESH)
    for d in range(1, R):
        pl.semaphore_signal(barrier, inc=1, device_id=(g, c, m, (r + d) % R), device_id_type=MESH)
    pl.semaphore_wait(barrier, length - 1 + G - 1 + R - 1)
    part = rows // R
    mine = pl.ds(pl.multiple_of(r * part, part), part)

    def kv_copy(d):
        return pltpu.make_async_remote_copy(
            src_ref=kv_hbm.at[mine], dst_ref=kvbuf.at[d, mine],
            send_sem=kv_send.at[d - 1], recv_sem=kv_recv.at[d - 1],
            device_id=at((place + d) % length), device_id_type=MESH,
        )

    def r_copy(e, d, back=0):
        owner = (r + R - back) % R
        piece = kvbuf.at[d, pl.ds(pl.multiple_of(owner * part, part), part)]
        return pltpu.make_async_remote_copy(
            src_ref=piece, dst_ref=piece,
            send_sem=r_send.at[e - 1, d - 1], recv_sem=r_recv.at[e - 1, d - 1],
            device_id=(g, c, m, (r + e) % R), device_id_type=MESH,
        )

    def w_copy(d, k):
        b = g * share + k
        return pltpu.make_async_remote_copy(
            src_ref=w_hbm.at[:, b], dst_ref=wbuf.at[:, b, m],
            send_sem=w_send.at[d - 1, k], recv_sem=w_recv.at[d - 1, k],
            device_id=(g, c, (m + d) % M, r), device_id_type=MESH,
        )

    def f_copy(e, d, k):
        b = g * share + k
        piece = wbuf.at[:, b, (m + M - d) % M]
        return pltpu.make_async_remote_copy(
            src_ref=piece, dst_ref=piece,
            send_sem=f_send.at[e - 1, d - 1, k], recv_sem=f_recv.at[e - 1, d - 1, k],
            device_id=((g + e) % G, c, m, r), device_id_type=MESH,
        )

    def f_arrival(e, d, k):
        b = ((g + G - e) % G) * share + k
        piece = wbuf.at[:, b, (m + M - d) % M]
        return pltpu.make_async_remote_copy(
            src_ref=piece, dst_ref=piece,
            send_sem=f_send.at[e - 1, d - 1, k], recv_sem=f_recv.at[e - 1, d - 1, k],
            device_id=((g + e) % G, c, m, r), device_id_type=MESH,
        )

    def w_arrival(d, k):
        b = g * share + k
        return pltpu.make_async_remote_copy(
            src_ref=w_hbm.at[:, b], dst_ref=wbuf.at[:, b, (m + M - d) % M],
            send_sem=w_send.at[d - 1, k], recv_sem=w_recv.at[d - 1, k],
            device_id=(g, c, (m + d) % M, r), device_id_type=MESH,
        )

    for d in range(1, slots):
        kv_copy(d).start()
    for k in range(share):
        for d in range(1, M):
            w_copy(d, k).start()

    e = jnp.exp(-decay_ref[...])
    s = e / (2.0 + e)
    s2 = s * s
    rate[...] = -16.0 * s * (1.0 + s2 * (1.0 / 3.0 + s2 * (1.0 / 5.0)))

    row = lax.broadcasted_iota(jnp.int32, (rows, rows), 0)
    col = lax.broadcasted_iota(jnp.int32, (rows, rows), 1)
    for d in range(slots):
        back = row - col + d * rows
        allowed = (back >= 0) & (back < WINDOW) & (place >= d)
        bias[:, d * rows : (d + 1) * rows] = jnp.where(allowed, 0.0, -1e30).astype(F32)

    groups8 = rows // 8
    sub = lax.broadcasted_iota(jnp.int32, (groups8, 8, bw), 1)

    def gates(b):
        lanes = pl.ds(pl.multiple_of(b * bw, bw), bw)
        xb = x_ref[:, lanes]
        g0 = jnp.dot(xb, wbuf[0, b].reshape(bw, bw), preferred_element_type=F32)
        g1 = jnp.dot(xb, wbuf[1, b].reshape(bw, bw), preferred_element_type=F32)
        y = rate[:, lanes] * jax.nn.sigmoid(g0)
        poly = 1.0 + y * (1 / 2 + y * (1 / 6 + y * (1 / 24 + y * (1 / 120 + y * (1 / 720)))))
        u = y * poly
        a = (1.0 + u).reshape(groups8, 8, bw)
        v = jnp.sqrt(-u * (2.0 + u)) * jax.nn.sigmoid(g1) * xb.astype(F32)
        v = v.reshape(groups8, 8, bw)
        for shift in (1, 2, 4):
            keep = sub >= shift
            before_v = jnp.where(keep, pltpu.roll(v, shift, 1), 0.0)
            before_a = jnp.where(keep, pltpu.roll(a, shift, 1), 1.0)
            v = a * before_v + v
            a = a * before_a
        decay_run[:, lanes] = a.reshape(rows, bw)
        state_run[:, lanes] = v.reshape(rows, bw)
        ta, tv = a[0, 7:8], v[0, 7:8]
        for k in range(1, groups8):
            tv = a[k, 7:8] * tv + v[k, 7:8]
            ta = a[k, 7:8] * ta
        total[0:1, lanes] = ta
        total[1:2, lanes] = tv

    scale = 1.0 / math.sqrt(hd)

    def head(h):
        lanes = pl.ds(pl.multiple_of(h * hd, hd), hd)
        keys = kvbuf[:, :, :hd].reshape(slots * rows, hd)
        values = kvbuf[:, :, hd:].reshape(slots * rows, hd)
        scores = lax.dot_general(
            q_ref[:, lanes], keys, (((1,), (1,)), ((), ())), preferred_element_type=F32
        )
        scores = scores * scale + bias[...]
        top = jnp.max(scores, axis=1, keepdims=True)
        weights = jnp.exp(scores - top)
        norm = jnp.sum(weights, axis=1, keepdims=True)
        out = jnp.dot(weights.astype(BF16), values, preferred_element_type=F32)
        att_ref[:, lanes] = (out / norm).astype(BF16)

    loads[1].wait()
    loads[2].wait()

    def direct(k, _):
        for d in range(1, M):
            w_arrival(d, k).wait_recv()
            for e in range(1, G):
                f_copy(e, d, k).start()
        gates(g * share + k)
        return 0

    lax.fori_loop(0, share // 2, direct, 0)

    def direct_head(k, _):
        head(k - share // 2)
        return direct(k, 0)

    for d in range(1, slots):
        kv_copy(d).wait_recv()
        for e in range(1, R):
            r_copy(e, d).start()

    loads[0].wait()
    loads[3].wait()
    for d in range(1, slots):
        for e in range(1, R):
            r_copy(e, d, e).wait_recv()
    lax.fori_loop(share // 2, share, direct_head, 0)
    first = share - share // 2

    stages = share * (G - 1)
    early = min(heads // 2, first + stages)

    def early_head(h, _):
        head(h)
        return 0

    for e in range(1, G):
        def relayed(k, _, e=e):
            stage = (e - 1) * share + k

            @pl.when(first + stage < early)
            def _():
                head(first + stage)

            for d in range(1, M):
                f_arrival(e, d, k).wait_recv()
            gates(((g + G - e) % G) * share + k)
            return 0

        lax.fori_loop(0, share, relayed, 0)

    def t_copy(d):
        return pltpu.make_async_remote_copy(
            src_ref=total, dst_ref=totals_in.at[d - 1],
            send_sem=t_send.at[d - 1], recv_sem=t_recv.at[d - 1],
            device_id=at((place + d) % length), device_id_type=MESH,
        )

    def t_start(d, _):
        t_copy(d).start()
        return 0

    lax.fori_loop(1, length, t_start, 0)
    lax.fori_loop(early, heads, early_head, 0)

    def t_fold(i, entering):
        d = length - 1 - i
        t_copy(d).wait_recv()
        new = totals_in[d - 1, 0:1] * entering + totals_in[d - 1, 1:2]
        return jnp.where(place >= d, new, entering)

    entering = lax.fori_loop(0, length - 1, t_fold, jnp.zeros((1, width), F32))

    def finish(k, entering):
        pieces = []
        for half in range(2):
            here = pl.ds(pl.multiple_of(k * 16 + half * 8, 8), 8)
            state = state_run[here] + decay_run[here] * entering
            entering = state[7:8]
            pieces.append(state)
        rec_ref[pl.ds(pl.multiple_of(k * 16, 16), 16)] = jnp.concatenate(pieces, axis=0).astype(BF16)
        return entering

    lax.fori_loop(0, rows // 16, finish, entering)

    for d in range(1, slots):
        kv_copy(d).wait_send()
        for e in range(1, R):
            r_copy(e, d).wait_send()

    def w_sent(k, _):
        for d in range(1, M):
            w_copy(d, k).wait_send()
            for e in range(1, G):
                f_copy(e, d, k).wait_send()
        return 0

    lax.fori_loop(0, share, w_sent, 0)

    def t_sent(d, _):
        t_copy(d).wait_send()
        return 0

    lax.fori_loop(1, length, t_sent, 0)


def on_device(lru_in, gate_weights, decay_param, queries, keys_values):
    G, C, M, R = (lax.axis_size(n) for n in ("groups", "ctx", "mp", "rep"))
    length = C * M
    rows, width = lru_in.shape
    _, blocks, depth, bw = gate_weights.shape
    share = blocks // G
    reach = min(WINDOW // rows, length - 1)
    slots = reach + 1
    dma = pltpu.SemaphoreType.DMA
    anywhere = pl.BlockSpec(memory_space=pltpu.HBM)
    vmem = pl.BlockSpec(memory_space=pltpu.VMEM)
    return pl.pallas_call(
        functools.partial(kernel, (G, C, M, R)),
        out_shape=(
            jax.ShapeDtypeStruct(lru_in.shape, BF16),
            jax.ShapeDtypeStruct(queries.shape, BF16),
        ),
        in_specs=[anywhere, anywhere, vmem, anywhere, anywhere],
        out_specs=(vmem, vmem),
        scratch_shapes=[
            pltpu.VMEM((rows, width), BF16),
            pltpu.VMEM((2, blocks, M, depth, bw), BF16),
            pltpu.VMEM(queries.shape, BF16),
            pltpu.VMEM((slots,) + keys_values.shape, BF16),
            pltpu.VMEM((rows, slots * rows), F32),
            pltpu.VMEM((1, width), F32),
            pltpu.VMEM((rows, width), F32),
            pltpu.VMEM((rows, width), F32),
            pltpu.VMEM((2, width), F32),
            pltpu.VMEM((length - 1, 2, width), F32),
            dma((4,)),
            dma((reach,)),
            dma((reach,)),
            dma((M - 1, share)),
            dma((M - 1, share)),
            dma((G - 1, M - 1, share)),
            dma((G - 1, M - 1, share)),
            dma((length - 1,)),
            dma((length - 1,)),
            dma((R - 1, reach)),
            dma((R - 1, reach)),
        ],
        compiler_params=pltpu.CompilerParams(
            collective_id=0, has_side_effects=True, vmem_limit_bytes=64 * 2**20 - 1048576
        ),
    )(lru_in, gate_weights, decay_param.reshape(1, width), queries, keys_values)


def solution(mesh):
    in_specs = (
        P(("groups", "ctx", "mp"), "rep"),
        P(None, "rep", "mp", None),
        P("rep"),
        P(("groups", "ctx", "mp"), "rep"),
        P(("groups", "ctx", "mp"), None),
    )
    out_specs = (P(("groups", "ctx", "mp"), "rep"), P(("groups", "ctx", "mp"), "rep"))
    return jax.shard_map(
        on_device, mesh=mesh, in_specs=in_specs, out_specs=out_specs, check_vma=False
    )
```
